512 devices in a mesh: seq: 128 (over z, y, core), grp: 4 (over x).
Axes of the slice: x: 4, y: 8, z: 8, core: 2. Of those that a mesh axis runs over, the one named last changes fastest.
Arguments:
- frames: bfloat16 [262144, 1024], P(('seq', 'grp')), may hold values from -6 to 6
- ln1_gain: float32 [1024], replicated, may hold values from 0.1 to 1.9
- w_in: bfloat16 [1024, 2, 1024], P('seq', None, 'grp'), may hold values from -0.1875 to 0.1875
- w_dw: bfloat16 [31, 1024], replicated, may hold values from -1 to 1
- ln2_gain: float32 [1024], replicated, may hold values from 0.1 to 1.9
- ln2_bias: float32 [1024], replicated, may hold values from -3 to 3
- w_out: bfloat16 [1024, 1024], P('grp', 'seq'), may hold values from -0.1875 to 0.1875
- block_utt: int32 [2048], replicated, may hold values from 0 to 511, as said below
- block_off: int32 [2048], replicated, may hold values from 0 to 6, as said below
- lengths: int32 [512], replicated, may hold values from 1 to 896, as said below
Outputs:
- result: bfloat16 [262144, 1024], P(('seq', 'grp'))
The draws below stay inside these ranges and needn't reach their ends.
Inputs may be any that keep to these rules, and one draw needn't show every extreme that they name: block_utt never falls along the blocks and names every utterance; each utterance is one run of 1 to 7 whole blocks, and some utterance has exactly 7. block_off counts the blocks of the run before a block, starting at 0. `lengths`: an utterance of n blocks has more than (n - 1) * 128 and at most n * 128 live frames.
All inputs are finite; a program needn't handle non-finite values.
Results may differ from the reference program's by a relative error of at most 0.0046.
Values may be sent and summed in bfloat16 or wider, within the bound.
No kernel may reach another device: no remote copies, remote signals or barrier semaphores. Data moves between devices by JAX's collectives and lax.ppermute only.
A program may use at most 64 MiB of HBM per device.

```python
import jax
import jax.numpy as jnp
from jax import lax

D = 1024
KER = 31
BLK = 128
FRAMES = 262144
NBLK = 2048
UTTS = 512
N_SEQ = 128


def layout_tables(key):
    base = jax.random.fold_in(key, 7)
    first_key, second_key = jax.random.split(base)
    pattern = jnp.array([-3, -2, -1, 0, 0, 1, 2, 3], jnp.int32)
    offsets = jnp.tile(pattern, UTTS // 8)
    order = jax.random.permutation(first_key, UTTS)
    counts = (4 + jnp.take(offsets, order)).astype(jnp.int32)
    ends = jnp.cumsum(counts).astype(jnp.int32)
    starts = (ends - counts).astype(jnp.int32)
    indices = jnp.arange(NBLK, dtype=jnp.int32)
    block_utt = jnp.sum((ends[None, :] <= indices[:, None]).astype(jnp.int32), axis=1).astype(jnp.int32)
    block_off = (indices - jnp.take(starts, block_utt)).astype(jnp.int32)
    tails = jax.random.randint(second_key, (UTTS,), 1, BLK + 1, dtype=jnp.int32)
    tails = jnp.where(counts == 7, BLK, tails).astype(jnp.int32)
    lengths = ((counts - 1) * BLK + tails).astype(jnp.int32)
    return (block_utt, block_off, lengths)


def draw_block_utt(key, part):
    return layout_tables(key)[0]


def draw_block_off(key, part):
    return layout_tables(key)[1]


def draw_lengths(key, part):
    return layout_tables(key)[2]


def shard_levels(rng, shape, shards, least, high):
    level = 1.0
    for dim, shards_of in shards:
        steps = jax.random.uniform(jax.random.fold_in(jax.random.fold_in(rng, 6), dim), (shards_of,), jnp.float32, least / len(shards), high / len(shards))
        level = level * jnp.repeat(jnp.exp(steps), shape[dim] // shards_of).reshape((-1,) + (1,) * (len(shape) - 1 - dim))
    return level


def noise(own_key, extent, scale, reach, cuts=(), held_as=jnp.bfloat16):
    loudness = shard_levels(own_key, extent, cuts, -0.22, 0.18) if cuts else 1.0
    values = jax.random.normal(own_key, extent, jnp.float32) * scale * loudness
    return jnp.minimum(jnp.maximum(values, -reach), reach).astype(held_as)


def setup_inputs(seed: int = 0) -> dict:
    key_of = jax.random.split(jax.random.key(seed), 11)
    return {
        "frames": noise(key_of[0], (FRAMES, D), 1.0, 6.0, ((0, 512),)),
        "ln1_gain": jnp.clip(1.0 + 0.18 * jax.random.normal(key_of[1], (D,), jnp.float32), 0.1, 1.9),
        "w_in": noise(key_of[2], (D, 2, D), D ** -0.5, 0.1875, ((0, 128), (2, 4))),
        "w_dw": noise(key_of[3], (KER, D), KER ** -0.5, 1.0),
        "ln2_gain": jnp.clip(1.0 + 0.18 * jax.random.normal(key_of[4], (D,), jnp.float32), 0.1, 1.9),
        "ln2_bias": noise(key_of[5], (D,), 0.5, 3.0, (), jnp.float32),
        "w_out": noise(key_of[6], (D, D), D ** -0.5, 0.1875, ((0, 4), (1, 128))),
        "block_utt": draw_block_utt(jax.random.fold_in(key_of[10], 71), 0),
        "block_off": draw_block_off(jax.random.fold_in(key_of[10], 71), 0),
        "lengths": draw_lengths(jax.random.fold_in(key_of[10], 71), 0),
    }


epsilon = 1e-05

def frame_keys(block_utt, block_off, lengths, first_row, row_count, margin):
    places = first_row - margin + jnp.arange(row_count + 2 * margin, dtype=jnp.int32)
    total_rows = block_utt.shape[0] * BLK
    inside = (places >= 0) & (places < total_rows)
    blocks = jnp.clip(places // BLK, 0, block_utt.shape[0] - 1)
    utterance = jnp.take(block_utt, blocks)
    position = jnp.take(block_off, blocks) * BLK + places % BLK
    living = inside & (position < jnp.take(lengths, utterance))
    return (jnp.where(living, utterance, -1), living[margin:margin + row_count])

def layer_norm(rows, gain):
    values = rows.astype(jnp.float32)
    average = lax.optimization_barrier(jnp.mean(values, axis=1, keepdims=True))
    centered = values - average
    spread = lax.optimization_barrier(jnp.mean(centered * centered, axis=1, keepdims=True))
    return (centered * lax.rsqrt(spread + epsilon) * gain).astype(jnp.bfloat16)

def gate_units(projected, living):
    half = projected.shape[1] // 2
    values = projected[:, :half] * jax.nn.sigmoid(projected[:, half:])
    return (values * living.astype(jnp.float32)[:, None]).astype(jnp.bfloat16)

def depthwise(widened, keys_wide, taps, row_count):
    margin = (taps.shape[0] - 1) // 2
    center = keys_wide[margin:margin + row_count]
    summed = jnp.zeros((row_count, widened.shape[1]), jnp.float32)
    for tap_index in range(taps.shape[0]):
        shifted = widened[tap_index:tap_index + row_count].astype(jnp.float32)
        same = (keys_wide[tap_index:tap_index + row_count] == center)[:, None]
        summed = summed + jnp.where(same, shifted, 0.0) * taps[tap_index].astype(jnp.float32)
    return summed

def finish(mixed, stat_sum, square_sum, width_total, gain, bias):
    average = stat_sum / width_total
    spread = square_sum / width_total - average * average
    normed = (mixed - average[:, None]) * lax.rsqrt(spread + epsilon)[:, None] * gain + bias
    return (normed * jax.nn.sigmoid(normed)).astype(jnp.bfloat16)

def reference(frames, ln1_gain, w_in, w_dw, ln2_gain, ln2_bias, w_out, block_utt, block_off, lengths):
    margin = (KER - 1) // 2
    keys_wide, living = frame_keys(block_utt, block_off, lengths, 0, FRAMES, margin)
    w_flat = w_in.reshape(D, 2 * D)

    def first_half(pair):
        rows, alive = pair
        normed = layer_norm(rows, ln1_gain)
        projected = jnp.dot(normed, w_flat, preferred_element_type=jnp.float32)
        return gate_units(projected, alive)
    gated = lax.map(first_half, (frames.reshape(N_SEQ, -1, D), living.reshape(N_SEQ, -1))).reshape(FRAMES, D)
    widened = jnp.pad(gated, ((margin, margin), (0, 0)))
    mixed = depthwise(widened, keys_wide, w_dw, FRAMES)

    def second_half(triple):
        rows, alive, mixed_rows = triple
        act = finish(mixed_rows, lax.optimization_barrier(jnp.sum(mixed_rows, axis=1)), lax.optimization_barrier(jnp.sum(mixed_rows * mixed_rows, axis=1)), float(D), ln2_gain, ln2_bias)
        output = jnp.dot(act, w_out, preferred_element_type=jnp.float32)
        return (rows.astype(jnp.float32) + output * alive.astype(jnp.float32)[:, None]).astype(jnp.bfloat16)
    result = lax.map(second_half, (frames.reshape(N_SEQ, -1, D), living.reshape(N_SEQ, -1), mixed.reshape(N_SEQ, -1, D)))
    return result.reshape(FRAMES, D)
```

```python
import jax
import jax.numpy as jnp
from jax import lax
from jax.experimental import pallas as pl
from jax.experimental.pallas import tpu as pltpu
from jax.sharding import Mesh
from jax.sharding import PartitionSpec as P

D = 1024
KER = 31
BLK = 128
EDGE = 16
WIN = BLK + 2 * EDGE
Z, YH, YL, C, X = 8, 4, 2, 2, 4
PART = D // X
ALL = ("z", "yh", "yl", "c", "x")
SEQ = ("z", "yh", "yl", "c")
epsilon = 1e-05


def sent_to_all(array, axes):
    size = lax.axis_size(axes)
    return lax.all_to_all(
        jnp.broadcast_to(array[None], (size, *array.shape)), axes, 0, 0, tiled=True
    )


def sigmoid(v):
    return 0.5 * jnp.tanh(0.5 * v) + 0.5


def normed_rows(rows, gain):
    values = rows.astype(jnp.float32)
    centered = values - jnp.mean(values, axis=1, keepdims=True)
    spread = jnp.mean(centered * centered, axis=1, keepdims=True)
    return (centered * lax.rsqrt(spread + epsilon) * gain).astype(jnp.bfloat16)


def module_kernel(
    place, utts, offs, lens, low_ref, frames_ref, high_ref, gain1_ref, taps_ref, gain2_ref, bias2_ref, own_ref,
    other_ref, out_ref, w_ref, normed_ref, gated_ref, mixed_ref, act_ref, taps32_ref, sems,
):
    rows = frames_ref.shape[0]
    blocks = rows // BLK
    core = place[1]

    def copies(x):
        found = []
        for source, half in ((own_ref, core), (other_ref, 1 - core)):
            for yl in range(YL):
                for yh in range(YH):
                    at = pl.multiple_of((yh * YL + yl) * (C * 8) + half * 8, 8)
                    found.append(
                        pltpu.make_async_copy(
                            source.at[yl, x, yh], w_ref.at[x, :, pl.ds(at, 8), :], sems.at[x]
                        )
                    )
        return found

    for x in range(X):
        for copy in copies(x):
            copy.start()

    gain1 = gain1_ref[...]
    normed_ref[:EDGE] = normed_rows(low_ref[...], gain1)
    for b in range(blocks):
        normed_ref[EDGE + b * BLK : EDGE + (b + 1) * BLK] = normed_rows(
            frames_ref[b * BLK : (b + 1) * BLK], gain1
        )
    normed_ref[EDGE + rows :] = normed_rows(high_ref[...], gain1)
    taps32_ref[...] = taps_ref[...].astype(jnp.float32)

    limits, firsts = [], []
    for b in range(blocks):
        at = place[0] + b
        off = offs[at]
        limits.append(lens[utts[at]] - off * BLK)
        firsts.append(jnp.where(off == 0, EDGE, 0))
    places = lax.broadcasted_iota(jnp.int32, (WIN, BLK), 0)

    for x in range(X):
        for copy in copies(x):
            copy.wait()
        w_v = w_ref[x, :, :, 0:PART].reshape(D, PART)
        w_g = w_ref[x, :, :, PART : 2 * PART].reshape(D, PART)
        values = jnp.dot(normed_ref[...], w_v, preferred_element_type=jnp.float32)
        gates = jnp.dot(normed_ref[...], w_g, preferred_element_type=jnp.float32)
        gated = (values * sigmoid(gates)).astype(jnp.bfloat16).astype(jnp.float32)
        for b in range(blocks):
            keep = (places >= firsts[b]) & (places < limits[b] + EDGE)
            for part in range(PART // 128):
                gated_ref[x * (PART // 128) + part, b] = jnp.where(
                    keep, gated[b * BLK : b * BLK + WIN, part * 128 : (part + 1) * 128], 0.0
                )

    def mix(step, carry):
        col, b = step // blocks, step % blocks
        lane = pl.multiple_of(col * 128, 128)
        total = jnp.zeros((BLK, 128), jnp.float32)
        for shift in range(8):
            window = gated_ref[col, b, pl.ds(shift, BLK + 24), :]
            for coarse in range(4):
                tap = 8 * coarse + shift - 1
                if tap >= 0:
                    total = total + window[8 * coarse : 8 * coarse + BLK] * taps32_ref[tap : tap + 1, pl.ds(lane, 128)]
        mixed_ref[col, b] = total
        return carry

    lax.fori_loop(0, (D // 128) * blocks, mix, 0)

    def settle(step, carry):
        b = step // 2
        half = pl.multiple_of((step % 2) * 64, 64)
        at = pl.multiple_of(step * 64, 64)
        first = mixed_ref[0, b, pl.ds(half, 64), :]
        total, squares = first, first * first
        for col in range(1, D // 128):
            piece = mixed_ref[col, b, pl.ds(half, 64), :]
            total = total + piece
            squares = squares + piece * piece
        average = jnp.sum(total, axis=1, keepdims=True) / float(D)
        spread = jnp.sum(squares, axis=1, keepdims=True) / float(D) - average * average
        scale = lax.rsqrt(spread + epsilon)
        for col in range(D // 128):
            lanes = slice(col * 128, (col + 1) * 128)
            piece = mixed_ref[col, b, pl.ds(half, 64), :]
            y = (piece - average) * scale * gain2_ref[:, lanes] + bias2_ref[:, lanes]
            act_ref[pl.ds(at, 64), lanes] = (y * sigmoid(y)).astype(jnp.bfloat16)
        return carry

    lax.fori_loop(0, rows // 64, settle, 0)

    per = D // X
    for n in range(X):
        output = jnp.zeros((rows, per), jnp.float32)
        for x in range(X):
            w_o = w_ref[x, 2 * n : 2 * n + 2, :, 2 * PART :].reshape(per, PART)
            output = output + lax.dot_general(
                act_ref[:, x * PART : (x + 1) * PART], w_o, (((1,), (1,)), ((), ())),
                preferred_element_type=jnp.float32,
            )
        lanes = slice(n * per, (n + 1) * per)
        for b in range(blocks):
            here = slice(b * BLK, (b + 1) * BLK)
            alive = lax.broadcasted_iota(jnp.int32, (BLK, per), 0) < limits[b]
            out_ref[here, lanes] = (
                frames_ref[here, lanes].astype(jnp.float32) + jnp.where(alive, output[here], 0.0)
            ).astype(jnp.bfloat16)


def per_device(
    frames, ln1_gain, w_in, w_dw, ln2_gain, ln2_bias, w_out, block_utt, block_off, lengths
):
    rows = frames.shape[0]
    count = lax.axis_size(ALL)
    up = [(i, i + 1) for i in range(count - 1)]
    low = lax.ppermute(frames[rows - EDGE :], ALL, up)
    high = lax.ppermute(frames[:EDGE], ALL, [(b, a) for a, b in up])

    held = jnp.concatenate([w_in.reshape(8, 2 * PART), w_out.T], axis=1)
    for axes in (("z",), ("yh",), ("yl", "x")):
        held = sent_to_all(held, axes)
        held = held.reshape(-1, *held.shape[-2:])
    held = held.reshape(YL, X, YH, Z, 8, 3 * PART)
    other = lax.ppermute(held, "c", [(0, 1), (1, 0)])

    place = jnp.stack([lax.axis_index(ALL) * (rows // BLK), lax.axis_index("c")]).astype(jnp.int32)
    vmem = pl.BlockSpec(memory_space=pltpu.VMEM)
    hbm = pl.BlockSpec(memory_space=pl.ANY)
    blocks = rows // BLK
    return pl.pallas_call(
        module_kernel,
        name="module",
        out_shape=jax.ShapeDtypeStruct((rows, D), jnp.bfloat16),
        grid_spec=pltpu.PrefetchScalarGridSpec(
            num_scalar_prefetch=4,
            grid=(),
            in_specs=[vmem] * 7 + [hbm] * 2,
            out_specs=vmem,
            scratch_shapes=[
                pltpu.VMEM((X, Z, YH * YL * C * 8, 3 * PART), jnp.bfloat16),
                pltpu.VMEM((rows + 2 * EDGE, D), jnp.bfloat16),
                pltpu.VMEM((D // 128, blocks, WIN, 128), jnp.float32),
                pltpu.VMEM((D // 128, blocks, BLK, 128), jnp.float32),
                pltpu.VMEM((rows, D), jnp.bfloat16),
                pltpu.VMEM((KER, D), jnp.float32),
                pltpu.SemaphoreType.DMA((X,)),
            ],
        ),
        compiler_params=pltpu.CompilerParams(vmem_limit_bytes=48 * 1024 * 1024),
        cost_estimate=pl.CostEstimate(flops=3 * 2 * rows * D * D, bytes_accessed=8 * 2**20, transcendentals=rows * D * 2),
    )(
        place, block_utt, block_off, lengths, low, frames, high, ln1_gain[None], w_dw, ln2_gain[None],
        ln2_bias[None], held, other,
    )


def solution(mesh):
    finer = Mesh(mesh.devices.reshape(Z, YH, YL, C, X), ALL)
    in_specs = (
        P(ALL, None), P(), P(SEQ, None, "x"), P(), P(), P(), P("x", SEQ), P(), P(), P(),
    )
    return jax.shard_map(
        per_device, mesh=finer, in_specs=in_specs, out_specs=P(ALL, None), check_vma=False
    )
```

```python
import jax
import jax.numpy as jnp
from jax import lax
from jax.experimental import pallas as pl
from jax.experimental.pallas import tpu as pltpu
from jax.sharding import Mesh
from jax.sharding import PartitionSpec as P

D = 1024
KER = 31
BLK = 128
EDGE = 16
WIN = BLK + 2 * EDGE
ZH, ZL, YH, YL, C, XH, XL = 4, 2, 4, 2, 2, 2, 2
X = XH * XL
PART = D // X
COLS = PART // 128
SPAN = 3 * PART
ALL = ("zh", "zl", "yh", "yl", "c", "xh", "xl")
SEQ = ("zh", "zl", "yh", "yl", "c")
epsilon = 1e-05


def repeated(array, axes):
    return jnp.broadcast_to(array[None], (lax.axis_size(axes), *array.shape))


def exchanged(array, axes):
    return lax.all_to_all(array, axes, 0, 0, tiled=True)


def from_next(array, axes, step):
    size = lax.axis_size(axes)
    return lax.ppermute(array, axes, [((i + step) % size, i) for i in range(size)])


def sigmoid(v):
    return 0.5 * jnp.tanh(0.5 * v) + 0.5


def normed_rows(rows, gain):
    values = rows.astype(jnp.float32)
    centered = values - jnp.mean(values, axis=1, keepdims=True)
    spread = jnp.mean(centered * centered, axis=1, keepdims=True)
    return (centered * lax.rsqrt(spread + epsilon) * gain).astype(jnp.bfloat16)


def weight_copies(own, other, held, sem, x):
    core = lax.axis_index("c")
    view = held.reshape(ZH, ZL, YH, YL, C, 8, held.shape[-1])
    return [
        pltpu.make_async_copy(source.at[yl, x], view.at[:, :, :, yl, half], sem)
        for source, half in ((own, core), (other, 1 - core))
        for yl in range(YL)
    ]


def norm_kernel(
    utts, offs, lens, low_ref, frames_ref, high_ref, gain1_ref, mine_ref, normed_hbm, marks_ref, outs_ref, normed_ref, staged_ref, sem, rows_sem
):
    staging = pltpu.make_async_copy(mine_ref.at[:, :, :, :, pl.ds(2 * PART, PART)], staged_ref, sem)
    staging.start()
    copies = [pltpu.make_async_copy(staged_ref, outs_ref.at[n], sem) for n in range(outs_ref.shape[0])]
    rows = frames_ref.shape[0]
    blocks = rows // BLK
    device = jnp.int32(0)
    for axis in ALL:
        device = device * lax.axis_size(axis) + lax.axis_index(axis)
    for b in range(blocks):
        at = device * blocks + b
        off = offs[at]
        marks_ref[b] = lens[utts[at]] - off * BLK
        marks_ref[blocks + b] = jnp.where(off == 0, EDGE, 0)
    staging.wait()
    for copy in copies:
        copy.start()
    gain1 = gain1_ref[...]
    normed_ref[:EDGE] = normed_rows(low_ref[...], gain1)
    for b in range(blocks):
        normed_ref[EDGE + b * BLK : EDGE + (b + 1) * BLK] = normed_rows(
            frames_ref[b * BLK : (b + 1) * BLK], gain1
        )
    normed_ref[EDGE + rows :] = normed_rows(high_ref[...], gain1)
    rows_copy = pltpu.make_async_copy(normed_ref, normed_hbm, rows_sem)
    rows_copy.start()
    for copy in copies:
        copy.wait()
    rows_copy.wait()


def pack_kernel(w_in_ref, w_out_ref, packed_ref):
    piece = jnp.concatenate([w_in_ref[:, 0, :], w_in_ref[:, 1, :], w_out_ref[...]], axis=1)
    for n in range(packed_ref.shape[0]):
        packed_ref[n] = piece


def mix_kernel(
    marks, taps_ref, gain2_ref, bias2_ref, normed_hbm, own_ref, other_ref, act_ref, normed_ref, held, gated_ref, mixed_ref, taps32_ref, sems
):
    rows = act_ref.shape[0]
    blocks = rows // BLK
    copies = [weight_copies(own_ref, other_ref, held.at[x], sems.at[x], x) for x in range(X)]
    rows_copy = pltpu.make_async_copy(normed_hbm, normed_ref, sems.at[X])
    rows_copy.start()
    for group in copies:
        for copy in group:
            copy.start()
    taps32_ref[...] = taps_ref[...].astype(jnp.float32)
    places = lax.broadcasted_iota(jnp.int32, (WIN, 128), 0)
    rows_copy.wait()
    for x in range(X):
        for copy in copies[x]:
            copy.wait()
        values = jnp.dot(normed_ref[...], held[x, :, 0:PART], preferred_element_type=jnp.float32)
        gates = jnp.dot(normed_ref[...], held[x, :, PART:], preferred_element_type=jnp.float32)
        gated = (values * sigmoid(gates)).astype(jnp.bfloat16).astype(jnp.float32)
        for b in range(blocks):
            keep = (places >= marks[blocks + b]) & (places < marks[b] + EDGE)
            for part in range(COLS):
                gated_ref[x * COLS + part, b] = jnp.where(
                    keep, gated[b * BLK : b * BLK + WIN, part * 128 : (part + 1) * 128], 0.0
                )

    def mix(step, carry):
        col, b = step // blocks, step % blocks
        lane = pl.multiple_of(col * 128, 128)
        total = jnp.zeros((BLK, 128), jnp.float32)
        for shift in range(8):
            window = gated_ref[col, b, pl.ds(shift, BLK + 24), :]
            for coarse in range(4):
                tap = 8 * coarse + shift - 1
                if tap >= 0:
                    total = total + window[8 * coarse : 8 * coarse + BLK] * taps32_ref[tap : tap + 1, pl.ds(lane, 128)]
        mixed_ref[col, b] = total
        return carry

    lax.fori_loop(0, (D // 128) * blocks, mix, 0, unroll=2)

    def settle(step, carry):
        b = step // 2
        half = pl.multiple_of((step % 2) * 64, 64)
        at = pl.multiple_of(step * 64, 64)
        total = mixed_ref[0, b, pl.ds(half, 64), :]
        squares = total * total
        for col in range(1, D // 128):
            piece = mixed_ref[col, b, pl.ds(half, 64), :]
            total = total + piece
            squares = squares + piece * piece
        average = jnp.sum(total, axis=1, keepdims=True) / float(D)
        spread = jnp.sum(squares, axis=1, keepdims=True) / float(D) - average * average
        scale = lax.rsqrt(spread + epsilon)
        for col in range(D // 128):
            lanes = slice(col * 128, (col + 1) * 128)
            piece = mixed_ref[col, b, pl.ds(half, 64), :]
            y = (piece - average) * scale * gain2_ref[:, lanes] + bias2_ref[:, lanes]
            act_ref[pl.ds(at, 64), lanes] = (y * sigmoid(y)).astype(jnp.bfloat16)
        return carry

    lax.fori_loop(0, rows // 64, settle, 0, unroll=True)


def out_kernel(marks, frames_ref, act_ref, own_ref, other_ref, out_ref, held, sem):
    rows = frames_ref.shape[0]
    blocks = rows // BLK
    copies = [copy for x in range(X) for copy in weight_copies(own_ref, other_ref, held.at[x], sem, x)]
    for copy in copies:
        copy.start()
    for copy in copies:
        copy.wait()
    per = D // 4
    for n in range(4):
        here = slice(n * per, (n + 1) * per)
        output = jnp.zeros((rows, per), jnp.float32)
        for x in range(X):
            output = output + lax.dot_general(
                act_ref[:, x * PART : (x + 1) * PART], held[x, here, :], (((1,), (1,)), ((), ())),
                preferred_element_type=jnp.float32,
            )
        for b in range(blocks):
            at = slice(b * BLK, (b + 1) * BLK)
            alive = lax.broadcasted_iota(jnp.int32, (BLK, per), 0) < marks[b]
            out_ref[at, here] = (
                frames_ref[at, here].astype(jnp.float32) + jnp.where(alive, output[at], 0.0)
            ).astype(jnp.bfloat16)


VMEM = pl.BlockSpec(memory_space=pltpu.VMEM)
SMEM = pl.BlockSpec(memory_space=pltpu.SMEM)
ANY = pl.BlockSpec(memory_space=pl.ANY)


def granted(mib):
    return pltpu.CompilerParams(vmem_limit_bytes=mib * 1024 * 1024)


def per_device(
    frames, ln1_gain, w_in, w_dw, ln2_gain, ln2_bias, w_out, block_utt, block_off, lengths
):
    rows = frames.shape[0]
    blocks = rows // BLK
    wide = rows + 2 * EDGE
    count = lax.axis_size(ALL)
    up = [(i, i + 1) for i in range(count - 1)]
    low = lax.ppermute(frames[rows - EDGE :], ALL, up)
    high = lax.ppermute(frames[:EDGE], ALL, [(b, a) for a, b in up])
    far, near = ("zh", "zl", "yh"), ("yl", "xh", "xl")
    packed = pl.pallas_call(
        pack_kernel,
        name="pack",
        out_shape=jax.ShapeDtypeStruct((ZH * ZL * YH, 8, SPAN), jnp.bfloat16),
        in_specs=[VMEM] * 2,
        out_specs=VMEM,
    )(w_in, w_out.T)
    mine = exchanged(packed, far).reshape(ZH, ZL, YH, 8, SPAN)
    normed, marks, outs = pl.pallas_call(
        norm_kernel,
        name="norm",
        out_shape=(
            jax.ShapeDtypeStruct((wide, D), jnp.bfloat16),
            jax.ShapeDtypeStruct((2 * blocks,), jnp.int32),
            jax.ShapeDtypeStruct((YL * X, ZH, ZL, YH, 8, PART), jnp.bfloat16),
        ),
        in_specs=[SMEM] * 3 + [VMEM] * 4 + [ANY],
        out_specs=(ANY, SMEM, ANY),
        scratch_shapes=[
            pltpu.VMEM((wide, D), jnp.bfloat16),
            pltpu.VMEM((ZH, ZL, YH, 8, PART), jnp.bfloat16),
            pltpu.SemaphoreType.DMA,
            pltpu.SemaphoreType.DMA,
        ],
        compiler_params=granted(8),
        cost_estimate=pl.CostEstimate(flops=8 * wide * D, bytes_accessed=4 * wide * D, transcendentals=wide),
    )(block_utt, block_off, lengths, low, frames, high, ln1_gain[None], mine)
    ins = exchanged(repeated(mine[..., : 2 * PART], near), near)
    ins, normed, outs = lax.optimization_barrier((ins, normed, outs))
    ins = ins.reshape(YL, X, ZH, ZL, YH, 8, 2 * PART)
    outs = exchanged(outs, near).reshape(YL, X, ZH, ZL, YH, 8, PART)
    ins_other = from_next(ins, "c", 1)
    act = pl.pallas_call(
        mix_kernel,
        name="mix",
        out_shape=jax.ShapeDtypeStruct((rows, D), jnp.bfloat16),
        in_specs=[SMEM] + [VMEM] * 3 + [ANY] * 3,
        out_specs=VMEM,
        scratch_shapes=[
            pltpu.VMEM((wide, D), jnp.bfloat16),
            pltpu.VMEM((X, D, 2 * PART), jnp.bfloat16),
            pltpu.VMEM((D // 128, blocks, WIN, 128), jnp.float32),
            pltpu.VMEM((D // 128, blocks, BLK, 128), jnp.float32),
            pltpu.VMEM((KER, D), jnp.float32),
            pltpu.SemaphoreType.DMA((X + 1,)),
        ],
        compiler_params=granted(16),
        cost_estimate=pl.CostEstimate(flops=16 * wide * D * D, bytes_accessed=16 * 2**20, transcendentals=2 * wide * D),
    )(marks, w_dw, ln2_gain[None], ln2_bias[None], pltpu.with_memory_space_constraint(normed, pltpu.HBM), ins, ins_other)
    outs, act = lax.optimization_barrier((outs, act))
    outs_other = from_next(outs, "c", 1)
    return pl.pallas_call(
        out_kernel,
        name="out",
        out_shape=jax.ShapeDtypeStruct((rows, D), jnp.bfloat16),
        in_specs=[SMEM] + [VMEM] * 2 + [ANY] * 2,
        out_specs=VMEM,
        scratch_shapes=[pltpu.VMEM((X, D, PART), jnp.bfloat16), pltpu.SemaphoreType.DMA],
        compiler_params=granted(10),
        cost_estimate=pl.CostEstimate(flops=2 * rows * D * D, bytes_accessed=5 * 2**20, transcendentals=0),
    )(marks, frames, act, outs, outs_other)


def solution(mesh):
    finer = Mesh(mesh.devices.reshape(ZH, ZL, YH, YL, C, XH, XL), ALL)
    grp = ("xh", "xl")
    in_specs = (
        P(ALL, None), P(), P(SEQ, None, grp), P(), P(), P(), P(grp, SEQ), P(), P(), P(),
    )
    return jax.shard_map(
        per_device, mesh=finer, in_specs=in_specs, out_specs=P(ALL, None), check_vma=False
    )
```
